32 devices in a mesh: team: 2 (over x), blk: 4 (over z), head: 4 (over y, core).
Axes of the slice: x: 2, y: 2, z: 4, core: 2. Of those that a mesh axis runs over, the one named last changes fastest.
Arguments:
- queries: bfloat16 [1024, 8, 8, 128], P('blk', 'head', 'team'), may hold values from -40 to 40
- features: bfloat16 [1024, 8192], P('blk', ('team', 'head')), may hold values from -6 to 6
- adapter_down: bfloat16 [4, 8192, 64], P(None, ('team', 'head')), may hold values from -0.0625 to 0.0625
- adapter_key_up: bfloat16 [4, 64, 8, 128], P(None, None, 'head'), may hold values from -0.75 to 0.75
- adapter_value_up: bfloat16 [4, 64, 8, 128], P(None, None, 'head'), may hold values from -0.75 to 0.75
- base_key: bfloat16 [1024, 8, 128], P('blk', 'head'), may hold values from -6 to 6
- base_value: bfloat16 [1024, 8, 128], P('blk', 'head'), may hold values from -24 to 24
- prefix_key: bfloat16 [2048, 8, 128], P('blk', 'head'), may hold values from -7 to 7
- prefix_value: bfloat16 [2048, 8, 128], P('blk', 'head'), may hold values from -24 to 24
- adapter_ids: int32 [4], replicated, may hold values from 0 to 3
- block_order: int32 [4], replicated, may hold values from 0 to 15
Outputs:
- attended: bfloat16 [1024, 8, 8, 128], P('blk', 'head', 'team')
The draws below stay inside these ranges and needn't reach their ends.
All inputs are finite; a program needn't handle non-finite values.
Results may differ from the reference program's by a relative error of at most 0.011.
Values may be sent and summed in bfloat16 or wider, within the bound.
No kernel may reach another device: no remote copies, remote signals or barrier semaphores. Data moves between devices by JAX's collectives and lax.ppermute only.
A program may use at most 64 MiB of HBM per device.

```python
import math
import jax
import jax.numpy as jnp
from jax import lax

D = 8192
KVH = 8
GROUP = 8
HD = 128
RANK = 64
ADAPTERS = 4
Q_DEV = 256
BLOCKS = 4
NEW = 1024
PREFIX = 2048


def drawn_draw(key):
    query_key, key_key = jax.random.split(jax.random.fold_in(key, 7301), 2)
    query_vals = jnp.clip(2.0 * jax.random.normal(query_key, (NEW, KVH, GROUP, HD), jnp.float32), -12.0, 12.0)
    key_vals = jnp.clip(jax.random.normal(key_key, (PREFIX, KVH, HD), jnp.float32), -6.0, 6.0)
    return (query_vals, key_vals)


def draw_queries(key, part):
    return drawn_draw(key)[0].astype(jnp.bfloat16)


def draw_prefix_key(key, part):
    return drawn_draw(key)[1].astype(jnp.bfloat16)


def plant(result, rng, least, largest):
    shape = result.shape
    index_at = [jax.random.randint(jax.random.fold_in(rng, axis), (), 0, shape[axis]) for axis in range(len(shape))]
    result = result.at[tuple(index_at)].set(least)
    longest = shape.index(max(shape))
    index_at[longest] = (index_at[longest] + 1) % shape[longest]
    return result.at[tuple(index_at)].set(largest)


def levels(rng, shape, cuts, least, top_value):
    loudness, own = 1.0, jax.random.fold_in(rng, 6)
    for dim, blocks in cuts:
        draws = jnp.exp(jax.random.uniform(jax.random.fold_in(own, dim), (blocks,), jnp.float32, least / len(cuts), top_value / len(cuts)))
        loudness = loudness * jnp.repeat(draws, shape[dim] // blocks).reshape([-1 if axis == dim else 1 for axis in range(len(shape))])
    return loudness


def centred(own_key, extent, spread, bound, shards=(), kind=jnp.bfloat16):
    values = spread * jax.random.normal(own_key, extent, jnp.float32)
    if shards:
        values = values * levels(own_key, extent, shards, -0.22, 0.18)
    return jnp.clip(values, -bound, bound).astype(kind)


def setup_inputs(seed: int = 0) -> dict:
    keys = jax.random.split(jax.random.key(seed), 12)
    queries = draw_queries(jax.random.fold_in(keys[11], 71), 0)
    features = centred(keys[1], (NEW, D), 1.0, 6.0, ((0, 4), (1, 8)))
    adapter_down = centred(keys[2], (ADAPTERS, D, RANK), D ** -0.5, 0.0625, ((1, 8),))
    adapter_key_up = centred(keys[3], (ADAPTERS, RANK, KVH, HD), RANK ** -0.5, 0.75, ((2, 4),))
    adapter_value_up = centred(keys[4], (ADAPTERS, RANK, KVH, HD), RANK ** -0.5, 0.75, ((2, 4),))
    base_key = centred(keys[5], (NEW, KVH, HD), 1.0, 6.0, ((0, 4), (1, 4)))
    base_value = centred(keys[6], (NEW, KVH, HD), 4.0, 24.0, ((0, 4), (1, 4)))
    prefix_key = draw_prefix_key(jax.random.fold_in(keys[11], 71), 0)
    prefix_value = centred(keys[8], (PREFIX, KVH, HD), 4.0, 24.0, ((0, 4), (1, 4)))
    adapter_ids = plant(jax.random.randint(keys[9], (BLOCKS,), 0, ADAPTERS), jax.random.fold_in(keys[9], 1), 0, ADAPTERS - 1).astype(jnp.int32)
    block_order = plant(jax.random.randint(keys[10], (BLOCKS,), 0, 4 * BLOCKS), jax.random.fold_in(keys[10], 1), 0, (4 * BLOCKS) - 1).astype(jnp.int32)
    return dict(queries=queries, features=features, adapter_down=adapter_down, adapter_key_up=adapter_key_up, adapter_value_up=adapter_value_up, base_key=base_key, base_value=base_value, prefix_key=prefix_key, prefix_value=prefix_value, adapter_ids=adapter_ids, block_order=block_order)


NEG_FILL = -1e+30

def reference(queries, features, adapter_down, adapter_key_up, adapter_value_up, base_key, base_value, prefix_key, prefix_value, adapter_ids, block_order):
    block_count = block_order.shape[0]
    highest = lax.Precision.HIGHEST
    token_index = jnp.arange(NEW, dtype=jnp.int32)
    query_pos = PREFIX + block_order[token_index // Q_DEV] * Q_DEV + token_index % Q_DEV
    key_pos = jnp.concatenate([jnp.arange(PREFIX, dtype=jnp.int32), query_pos])
    down_rows = adapter_down[adapter_ids].astype(jnp.float32)
    grouped = features.reshape(block_count, Q_DEV, D).astype(jnp.float32)
    latent = jnp.einsum('btd,bdr->btr', grouped, down_rows, precision=highest)
    latent_wide = lax.optimization_barrier(latent.astype(jnp.bfloat16)).astype(jnp.float32)

    def expand(up_table, base_rows):
        up_rows = up_table[adapter_ids].reshape(block_count, RANK, KVH * HD).astype(jnp.float32)
        delta = jnp.einsum('btr,bre->bte', latent_wide, up_rows, precision=highest).reshape(NEW, KVH, HD)
        return (base_rows.astype(jnp.float32) + delta).astype(jnp.bfloat16)
    key_rows = jnp.concatenate([prefix_key, expand(adapter_key_up, base_key)], axis=0)
    value_rows = jnp.concatenate([prefix_value, expand(adapter_value_up, base_value)], axis=0)
    score_scale = 1.0 / math.sqrt(HD)

    def one_head(head_index):
        head_keys = lax.dynamic_index_in_dim(key_rows, head_index, 1, keepdims=False).astype(jnp.float32)
        head_values = lax.dynamic_index_in_dim(value_rows, head_index, 1, keepdims=False).astype(jnp.float32)
        head_queries = lax.dynamic_index_in_dim(queries, head_index, 1, keepdims=False)

        def one_block(block_index):
            block_queries = lax.dynamic_slice_in_dim(head_queries, block_index * Q_DEV, Q_DEV, 0).astype(jnp.float32)
            block_pos = lax.dynamic_slice_in_dim(query_pos, block_index * Q_DEV, Q_DEV, 0)
            scores = jnp.einsum('tgd,sd->gts', block_queries, head_keys, precision=highest) * score_scale
            visible = key_pos[None, None, :] <= block_pos[None, :, None]
            scores = jnp.where(visible, scores, NEG_FILL)
            row_max = lax.optimization_barrier(jnp.max(scores, axis=-1, keepdims=True))
            weights = jnp.where(visible, jnp.exp(scores - row_max), 0.0)
            row_sum = lax.optimization_barrier(jnp.sum(weights, axis=-1))
            rounded = lax.optimization_barrier(weights.astype(jnp.bfloat16)).astype(jnp.float32)
            mixed = jnp.einsum('gts,sd->gtd', rounded, head_values, precision=highest)
            return (mixed / row_sum[..., None]).astype(jnp.bfloat16)
        return lax.map(one_block, jnp.arange(block_count, dtype=jnp.int32))
    stacked = lax.map(one_head, jnp.arange(KVH, dtype=jnp.int32))
    return stacked.transpose(1, 3, 0, 2, 4).reshape(NEW, KVH, GROUP, HD)
```

```python
import functools
import math

import jax
import jax.numpy as jnp
from jax import lax
from jax.experimental import pallas as pl
from jax.experimental.pallas import tpu as pltpu
from jax.sharding import PartitionSpec as P


NEG_FILL = -1e30
LOG2E = 1.4426950408889634


def dot_t(a, b):
    return lax.dot_general(a, b, (((1,), (1,)), ((), ())), preferred_element_type=jnp.float32)


def prefix_kernel(scale, tile, pieces, *refs):
    q_refs = refs[:2]
    kv_refs = refs[2 : 2 + pieces]
    outs = refs[2 + pieces :]
    half = kv_refs[0].shape[0] // 2
    rows = q_refs[0].shape[0]
    for side in range(2):
        q_ref = q_refs[side]
        m_ref, l_ref, acc_ref = outs[3 * side : 3 * side + 3]

        def body(i, _):
            at = pl.ds(pl.multiple_of(i * tile, tile), tile)
            q = q_ref[at, :]
            scores = [dot_t(q, kv[:half, :]) for kv in kv_refs]
            top = functools.reduce(jnp.maximum, [jnp.max(s, axis=1, keepdims=True) for s in scores])
            top = top * scale
            total = jnp.zeros((tile, 1), jnp.float32)
            acc = jnp.zeros((tile, q.shape[1]), jnp.float32)
            for s, kv in zip(scores, kv_refs):
                p = jnp.exp2(s * scale - top)
                total = total + jnp.sum(p, axis=1, keepdims=True)
                acc = acc + jnp.dot(
                    p.astype(jnp.bfloat16), kv[half:, :], preferred_element_type=jnp.float32
                )
            m_ref[at, :] = jnp.broadcast_to(top, (tile, 128))
            l_ref[at, :] = jnp.broadcast_to(total, (tile, 128))
            acc_ref[at, :] = acc
            return 0

        lax.fori_loop(0, rows // tile, body, 0, unroll=2)


def prefix_attend(q_pair, pieces, scale):
    rows, head_dim = q_pair[0].shape
    tile = 128
    state = [
        jax.ShapeDtypeStruct((rows, 128), jnp.float32),
        jax.ShapeDtypeStruct((rows, 128), jnp.float32),
        jax.ShapeDtypeStruct((rows, head_dim), jnp.float32),
    ]
    keys = sum(p.shape[0] // 2 for p in pieces)
    out = pl.pallas_call(
        functools.partial(prefix_kernel, scale, tile, len(pieces)),
        out_shape=state * 2,
        in_specs=[pl.BlockSpec(memory_space=pltpu.VMEM)] * (2 + len(pieces)),
        out_specs=[pl.BlockSpec(memory_space=pltpu.VMEM)] * 6,
        cost_estimate=pl.CostEstimate(
            flops=8 * rows * keys * head_dim,
            bytes_accessed=rows * head_dim * 16,
            transcendentals=2 * rows * keys,
        ),
        name="prefix_attend",
    )(*q_pair, *pieces)
    return out[:3], out[3:]


def new_kernel(scale, tile, pieces, group, *refs):
    delta_ref, q_ref, m_ref, l_ref, acc_ref = refs[:5]
    kv_refs = refs[5 : 5 + pieces]
    out_ref = refs[5 + pieces]
    half = kv_refs[0].shape[0] // 2
    rows = q_ref.shape[0]

    def body(i, _):
        at = pl.ds(pl.multiple_of(i * tile, tile), tile)
        q = q_ref[at, :]
        token = (lax.broadcasted_iota(jnp.int32, (tile, half), 0) + i * tile) // group
        ahead = lax.broadcasted_iota(jnp.int32, (tile, half), 1) - token
        top = m_ref[at, :][:, :1]
        start = top
        scores = []
        for n, kv in enumerate(kv_refs):
            s = dot_t(q, kv[:half, :]) * scale
            s = jnp.where(ahead <= delta_ref[n], s, NEG_FILL)
            top = jnp.maximum(top, jnp.max(s, axis=1, keepdims=True))
            scores.append(s)
        factor = jnp.exp2(start - top)
        total = l_ref[at, :][:, :1] * factor
        acc = acc_ref[at, :] * factor
        for s, kv in zip(scores, kv_refs):
            p = jnp.exp2(s - top)
            total = total + jnp.sum(p, axis=1, keepdims=True)
            acc = acc + jnp.dot(
                p.astype(jnp.bfloat16), kv[half:, :], preferred_element_type=jnp.float32
            )
        out_ref[at, :] = (acc / total).astype(out_ref.dtype)
        return 0

    lax.fori_loop(0, rows // tile, body, 0, unroll=2)


def new_attend(delta, q, state, pieces, scale, group):
    rows, head_dim = q.shape
    keys = sum(p.shape[0] // 2 for p in pieces)
    return pl.pallas_call(
        functools.partial(new_kernel, scale, 128, len(pieces), group),
        out_shape=jax.ShapeDtypeStruct((rows, head_dim), jnp.bfloat16),
        in_specs=[pl.BlockSpec(memory_space=pltpu.SMEM)]
        + [pl.BlockSpec(memory_space=pltpu.VMEM)] * (4 + len(pieces)),
        out_specs=pl.BlockSpec(memory_space=pltpu.VMEM),
        cost_estimate=pl.CostEstimate(
            flops=4 * rows * keys * head_dim,
            bytes_accessed=rows * head_dim * 16,
            transcendentals=rows * keys,
        ),
        name="new_attend",
    )(delta, q, *state, *pieces)


def butterfly_sum(value, axis):
    size = lax.axis_size(axis)
    if size & (size - 1):
        return lax.psum(value, axis)
    step = 1
    while step < size:
        value = value + lax.ppermute(value, axis, [(i, i ^ step) for i in range(size)])
        step *= 2
    return value


def on_device(
    queries,
    features,
    adapter_down,
    adapter_key_up,
    adapter_value_up,
    base_key,
    base_value,
    prefix_key,
    prefix_value,
    adapter_ids,
    block_order,
):
    block_count = lax.axis_size("blk")
    team_count = lax.axis_size("team")
    my_block = lax.axis_index("blk")
    query_dev, kv_heads, group_dev, head_dim = queries.shape
    chosen = adapter_ids[my_block]
    mine = lax.axis_index("team") % 2
    scale = LOG2E / math.sqrt(head_dim)

    def swap(value):
        return lax.ppermute(value, "team", [(i, i ^ 1) for i in range(team_count)])

    def pick(array, axis, other=False):
        index = 1 - mine if other else mine
        return lax.dynamic_index_in_dim(array, index, axis, keepdims=False)

    def shifted(value, step):
        perm = [(i, (i + step) % block_count) for i in range(block_count)]
        return lax.ppermute(value, "blk", perm)

    own_prefix = jnp.concatenate([pick(prefix_key, 1), pick(prefix_value, 1)], axis=0)
    rows = query_dev * group_dev
    far_prefix = [shifted(own_prefix, step) for step in range(1, block_count)]
    own_queries = pick(queries, 1).reshape(rows, head_dim)
    swapped_queries = swap(pick(queries, 1, True).reshape(rows, head_dim))

    down_rows = lax.dynamic_index_in_dim(adapter_down, chosen, 0, keepdims=False)
    partial_latent = jnp.dot(features, down_rows, preferred_element_type=jnp.float32)
    latent = butterfly_sum(butterfly_sum(partial_latent, "head"), "team").astype(jnp.bfloat16)

    def expand(up_table, base_rows):
        up_rows = pick(lax.dynamic_index_in_dim(up_table, chosen, 0, keepdims=False), 1)
        delta = jnp.dot(latent, up_rows, preferred_element_type=jnp.float32)
        return (pick(base_rows, 1).astype(jnp.float32) + delta).astype(jnp.bfloat16)

    own_new = jnp.concatenate(
        [expand(adapter_key_up, base_key), expand(adapter_value_up, base_value)], axis=0
    )
    far_new = [shifted(own_new, step) for step in range(1, block_count)]
    sources = (my_block - jnp.arange(block_count, dtype=jnp.int32)) % block_count
    delta = (block_order[my_block] - block_order[sources]) * query_dev

    own_state, swapped_state = prefix_attend(
        (own_queries, swapped_queries), [own_prefix] + far_prefix, scale
    )
    new_pieces = [own_new] + far_new
    swapped_out = new_attend(delta, swapped_queries, swapped_state, new_pieces, scale, group_dev)
    other_out = swap(swapped_out)
    own_out = new_attend(delta, own_queries, own_state, new_pieces, scale, group_dev)
    shape = (query_dev, group_dev, head_dim)
    own_out = own_out.reshape(shape)
    other_out = other_out.reshape(shape)
    first = jnp.where(mine == 0, own_out, other_out)
    second = jnp.where(mine == 0, other_out, own_out)
    return jnp.stack([first, second], axis=1)


def solution(mesh):
    placed = (
        P("blk", "head", "team", None),
        P("blk", ("team", "head")),
        P(None, ("team", "head"), None),
        P(None, None, "head", None),
        P(None, None, "head", None),
        P("blk", "head", None),
        P("blk", "head", None),
        P("blk", "head", None),
        P("blk", "head", None),
        P(),
        P(),
    )
    return jax.shard_map(
        on_device,
        mesh=mesh,
        in_specs=placed,
        out_specs=P("blk", "head", "team", None),
        check_vma=False,
    )
```

```python
import functools
import math

import jax
import jax.numpy as jnp
from jax import lax
from jax.experimental import pallas as pl
from jax.experimental.pallas import tpu as pltpu
from jax.sharding import PartitionSpec as P


NEG_FILL = -1e30
LOG2E = 1.4426950408889634
TILE = 128
LIMIT = 20 * 2**20
VMEM = pl.BlockSpec(memory_space=pltpu.VMEM)
SMEM = pl.BlockSpec(memory_space=pltpu.SMEM)


def dot_t(a, b):
    return lax.dot_general(a, b, (((1,), (1,)), ((), ())), preferred_element_type=jnp.float32)


def latent_kernel(ids_ref, features_ref, down_ref, out_ref, held, sem):
    chosen = ids_ref[lax.axis_index("blk")]
    copy = pltpu.make_async_copy(down_ref.at[chosen], held, sem)
    copy.start()
    copy.wait()
    out_ref[...] = dot_t(held[...], features_ref[...])


def partial_latent(ids, features, down):
    tokens, depth = features.shape
    rank = down.shape[1]
    return pl.pallas_call(
        latent_kernel,
        out_shape=jax.ShapeDtypeStruct((rank, tokens), jnp.float32),
        in_specs=[SMEM, VMEM, pl.BlockSpec(memory_space=pl.ANY)],
        out_specs=VMEM,
        scratch_shapes=[pltpu.VMEM((rank, depth), down.dtype), pltpu.SemaphoreType.DMA(())],
        compiler_params=pltpu.CompilerParams(vmem_limit_bytes=LIMIT),
        cost_estimate=pl.CostEstimate(
            flops=2 * tokens * depth * rank,
            bytes_accessed=2 * depth * (tokens + rank),
            transcendentals=0,
        ),
        name="partial_latent",
    )(ids, features, down)


def expand_kernel(ids_ref, first, second, key_up, value_up, key_base, value_base, out_ref):
    chosen = ids_ref[lax.axis_index("blk")]
    latent = (first[...] + second[...]).astype(jnp.bfloat16)
    tokens = key_base.shape[0]
    for n, (up, base) in enumerate(((key_up, key_base), (value_up, value_base))):
        delta = lax.dot_general(
            latent, up[chosen], (((0,), (0,)), ((), ())), preferred_element_type=jnp.float32
        )
        out_ref[n * tokens : (n + 1) * tokens, :] = (
            base[...].astype(jnp.float32) + delta
        ).astype(jnp.bfloat16)


def expand(ids, first, second, key_up, value_up, key_base, value_base):
    tokens, head_dim = key_base.shape
    return pl.pallas_call(
        expand_kernel,
        out_shape=jax.ShapeDtypeStruct((2 * tokens, head_dim), jnp.bfloat16),
        in_specs=[SMEM] + [VMEM] * 6,
        out_specs=VMEM,
        compiler_params=pltpu.CompilerParams(vmem_limit_bytes=LIMIT),
        cost_estimate=pl.CostEstimate(
            flops=4 * tokens * head_dim * first.shape[0],
            bytes_accessed=8 * tokens * head_dim,
            transcendentals=0,
        ),
        name="expand",
    )(ids, first, second, key_up, value_up, key_base, value_base)


def attend_kernel(sides, masks, carried, final, group, scale, *refs):
    order_ref, refs = refs[0], refs[1:]
    q_refs, refs = refs[:sides], refs[sides:]
    state_refs, refs = refs[: 2 * sides * carried], refs[2 * sides * carried :]
    kv_refs, outs = refs[: len(masks)], refs[len(masks) :]
    head_dim = q_refs[0].shape[1]
    rows = q_refs[0].shape[0]
    me = lax.axis_index("blk")

    def bound(mask, length):
        return (order_ref[me] - order_ref[me ^ mask]) * (length * group)

    bounds = [
        None if mask is None else bound(mask, kv.shape[0] // 2)
        for mask, kv in zip(masks, kv_refs)
    ]

    for side in range(sides):

        def body(i, _):
            at = pl.ds(pl.multiple_of(i * TILE, TILE), TILE)
            q = q_refs[side][at, :]
            scores = []
            top = None
            for kv, limit in zip(kv_refs, bounds):
                half = kv.shape[0] // 2
                s = dot_t(q, kv[:half, :])
                if limit is not None:
                    ahead = lax.broadcasted_iota(jnp.int32, (TILE, half), 1) * group
                    ahead = ahead - lax.broadcasted_iota(jnp.int32, (TILE, half), 0)
                    s = jnp.where(ahead <= limit + i * TILE, s, NEG_FILL)
                scores.append(s)
                most = jnp.max(s, axis=1, keepdims=True)
                top = most if top is None else jnp.maximum(top, most)
            top = jnp.broadcast_to(top * scale, (TILE, head_dim))
            acc = None
            if carried:
                old = state_refs[2 * side][at, :]
                top = jnp.maximum(top, old)
                factor = jnp.exp2(old - top)
                acc = state_refs[2 * side + 1][at, :] * jnp.concatenate([factor, factor], axis=1)
            for s, kv in zip(scores, kv_refs):
                half = kv.shape[0] // 2
                p = jnp.exp2(s * scale - top[:, :1])
                values = kv[half:, :]
                values = jnp.concatenate([values, jnp.ones_like(values)], axis=1)
                part = jnp.dot(p.astype(jnp.bfloat16), values, preferred_element_type=jnp.float32)
                acc = part if acc is None else acc + part
            if final:
                outs[side][at, :] = (acc[:, :head_dim] / acc[:, head_dim:]).astype(jnp.bfloat16)
            else:
                outs[2 * side][at, :] = top
                outs[2 * side + 1][at, :] = acc
            return 0

        lax.fori_loop(0, rows // TILE, body, 0, unroll=min(8, rows // TILE))


def attend(order, queries, states, pieces, final, group, scale):
    sides = len(queries)
    rows, head_dim = queries[0].shape
    masks = tuple(mask for mask, _ in pieces)
    keys = sum(piece.shape[0] // 2 for _, piece in pieces)
    if final:
        shapes = [jax.ShapeDtypeStruct((rows, head_dim), jnp.bfloat16)] * sides
    else:
        shapes = [
            jax.ShapeDtypeStruct((rows, head_dim), jnp.float32),
            jax.ShapeDtypeStruct((rows, 2 * head_dim), jnp.float32),
        ] * sides
    carried = states is not None
    operands = [*queries, *(states or []), *(piece for _, piece in pieces)]
    return pl.pallas_call(
        functools.partial(attend_kernel, sides, masks, carried, final, group, scale),
        out_shape=shapes,
        in_specs=[SMEM] + [VMEM] * len(operands),
        out_specs=[VMEM] * len(shapes),
        compiler_params=pltpu.CompilerParams(vmem_limit_bytes=LIMIT),
        cost_estimate=pl.CostEstimate(
            flops=6 * sides * rows * keys * head_dim,
            bytes_accessed=sides * rows * head_dim * 4,
            transcendentals=sides * rows * keys,
        ),
        name="attend",
    )(order, *operands)


def butterfly(value, axis, size, keep_last=False):
    step = 1
    pair = None
    while step < size:
        if pair is not None:
            value = pair[0] + pair[1]
        pair = (value, lax.ppermute(value, axis, [(i, i ^ step) for i in range(size)]))
        step *= 2
    return pair if keep_last else pair[0] + pair[1]


def gather_blocks(value, count):
    held = {0: value}
    step = count // 2
    while step:
        perm = [(i, i ^ step) for i in range(count)]
        for mask in list(held):
            held[mask ^ step] = lax.ppermute(held[mask], "blk", perm)
        step //= 2
    return held


def on_device(
    queries,
    features,
    adapter_down,
    adapter_key_up,
    adapter_value_up,
    base_key,
    base_value,
    prefix_key,
    prefix_value,
    adapter_ids,
    block_order,
):
    block_count = lax.axis_size("blk")
    team_count = lax.axis_size("team")
    query_dev, kv_heads, group_dev, head_dim = queries.shape
    mine = lax.axis_index("team") & 1
    scale = LOG2E / math.sqrt(head_dim)
    rows = query_dev * group_dev

    def swap(value):
        return lax.ppermute(value, "team", [(i, i ^ 1) for i in range(team_count)])

    def pick(array, axis, other=False):
        index = 1 - mine if other else mine
        return lax.dynamic_index_in_dim(array, index, axis, keepdims=False)

    latent = partial_latent(adapter_ids, features, jnp.swapaxes(adapter_down, 1, 2))
    latent = butterfly(latent, "head", lax.axis_size("head"))
    first, second = butterfly(latent, "team", team_count, True)

    own_prefix = jnp.concatenate([pick(prefix_key, 1), pick(prefix_value, 1)], axis=0)
    prefix = gather_blocks(own_prefix, block_count)
    own_queries = pick(queries, 1).reshape(rows, head_dim)
    far_queries = swap(pick(queries, 1, True).reshape(rows, head_dim))
    own_new = expand(
        adapter_ids,
        first,
        second,
        pick(adapter_key_up, 2),
        pick(adapter_value_up, 2),
        pick(base_key, 1),
        pick(base_value, 1),
    )
    new = gather_blocks(own_new, block_count)

    last = block_count - 1
    both = [own_queries, far_queries]
    early = [(None, piece) for mask, piece in prefix.items() if mask != last]
    state = attend(block_order, both, None, early, False, group_dev, scale)
    late = [(None, prefix[last])] + [(mask, piece) for mask, piece in new.items() if mask != last]
    state = attend(block_order, both, state, late, False, group_dev, scale)
    tail = [(last, new[last])]
    far_out = attend(block_order, both[1:], state[2:], tail, True, group_dev, scale)[0]
    received = swap(far_out)
    own_out = attend(block_order, both[:1], state[:2], tail, True, group_dev, scale)[0]
    shape = (query_dev, 1, group_dev, head_dim)
    head = lax.broadcasted_iota(jnp.int32, queries.shape, 1)
    return jnp.where(head == mine, own_out.reshape(shape), received.reshape(shape))


def solution(mesh):
    placed = (
        P("blk", "head", "team", None),
        P("blk", ("team", "head")),
        P(None, ("team", "head"), None),
        P(None, None, "head", None),
        P(None, None, "head", None),
        P("blk", "head", None),
        P("blk", "head", None),
        P("blk", "head", None),
        P("blk", "head", None),
        P(),
        P(),
    )
    return jax.shard_map(
        on_device,
        mesh=mesh,
        in_specs=placed,
        out_specs=P("blk", "head", "team", None),
        check_vma=False,
    )
```

```python
import functools
import math

import jax
import jax.numpy as jnp
from jax import lax
from jax.experimental import pallas as pl
from jax.experimental.pallas import tpu as pltpu
from jax.sharding import PartitionSpec as P


NEG_FILL = -1e30
LOG2E = 1.4426950408889634
TILE = 128
UNROLL = 8
LIMIT = 20 * 2**20
VMEM = pl.BlockSpec(memory_space=pltpu.VMEM)
SMEM = pl.BlockSpec(memory_space=pltpu.SMEM)


def dot_t(a, b):
    return lax.dot_general(a, b, (((1,), (1,)), ((), ())), preferred_element_type=jnp.float32)


def latent_kernel(ids_ref, _, features_ref, down_ref, out_ref, held, sem):
    chosen = ids_ref[lax.axis_index("blk")]
    copy = pltpu.make_async_copy(down_ref.at[chosen], held, sem)
    copy.start()
    copy.wait()
    out_ref[...] = dot_t(held[...], features_ref[...])


def partial_latent(ids, order, features, down):
    tokens, depth = features.shape
    rank = down.shape[1]
    return pl.pallas_call(
        latent_kernel,
        out_shape=jax.ShapeDtypeStruct((rank, tokens), jnp.float32),
        in_specs=[SMEM, SMEM, VMEM, pl.BlockSpec(memory_space=pl.ANY)],
        out_specs=VMEM,
        scratch_shapes=[pltpu.VMEM((rank, depth), down.dtype), pltpu.SemaphoreType.DMA(())],
        compiler_params=pltpu.CompilerParams(vmem_limit_bytes=LIMIT),
        cost_estimate=pl.CostEstimate(
            flops=2 * tokens * depth * rank,
            bytes_accessed=2 * depth * (tokens + rank),
            transcendentals=0,
        ),
        name="partial_latent",
    )(ids, order, features, down)


def expand_kernel(ids_ref, first, second, key_up, value_up, key_base, value_base, out_ref):
    chosen = ids_ref[lax.axis_index("blk")]
    latent = (first[...] + second[...]).astype(jnp.bfloat16)
    tokens = key_base.shape[0]
    for n, (up, base) in enumerate(((key_up, key_base), (value_up, value_base))):
        delta = lax.dot_general(
            latent, up[chosen], (((0,), (0,)), ((), ())), preferred_element_type=jnp.float32
        )
        out_ref[n * tokens : (n + 1) * tokens, :] = (
            base[...].astype(jnp.float32) + delta
        ).astype(jnp.bfloat16)


def expand(ids, first, second, key_up, value_up, key_base, value_base):
    tokens, head_dim = key_base.shape
    return pl.pallas_call(
        expand_kernel,
        out_shape=jax.ShapeDtypeStruct((2 * tokens, head_dim), jnp.bfloat16),
        in_specs=[SMEM] + [VMEM] * 6,
        out_specs=VMEM,
        compiler_params=pltpu.CompilerParams(vmem_limit_bytes=LIMIT),
        cost_estimate=pl.CostEstimate(
            flops=4 * tokens * head_dim * first.shape[0],
            bytes_accessed=8 * tokens * head_dim,
            transcendentals=0,
        ),
        name="expand",
    )(ids, first, second, key_up, value_up, key_base, value_base)


def wide(value, width):
    return jnp.concatenate([value] * (width // value.shape[1]), axis=1)


def attend_kernel(span, masks, carried, final, group, scale, *refs):
    order_ref, refs = (None, refs) if set(masks) == {None} else (refs[0], refs[1:])
    q_ref, refs = refs[0], refs[1:]
    state_refs, refs = refs[: 2 * carried], refs[2 * carried :]
    kv_refs, outs = refs[: len(masks)], refs[len(masks) :]
    head_dim = q_ref.shape[1]
    start, rows = span
    me = lax.axis_index("blk")
    bounds = [
        None
        if mask is None
        else (order_ref[me] - order_ref[me ^ mask]) * (kv.shape[0] // 2 * group)
        for mask, kv in zip(masks, kv_refs)
    ]

    def body(i, _):
        here = pl.ds(pl.multiple_of(i * TILE, TILE), TILE)
        at = pl.ds(pl.multiple_of(start + i * TILE, TILE), TILE)
        q = q_ref[at, :]
        scores = []
        top = None
        for kv, limit in zip(kv_refs, bounds):
            half = kv.shape[0] // 2
            s = dot_t(q, kv[:half, :])
            if limit is not None:
                ahead = lax.broadcasted_iota(jnp.int32, (TILE, half), 1) * group
                ahead = ahead - lax.broadcasted_iota(jnp.int32, (TILE, half), 0)
                s = jnp.where(ahead <= limit + (start + i * TILE), s, NEG_FILL)
            scores.append(s)
            most = jnp.max(s, axis=1, keepdims=True)
            top = most if top is None else jnp.maximum(top, most)
        top = jnp.broadcast_to(top * scale, (TILE, head_dim))
        acc = None
        if carried:
            old = state_refs[0][at, :]
            top = jnp.maximum(top, old)
            acc = state_refs[1][at, :] * wide(jnp.exp2(old - top), 2 * head_dim)
        for s, kv in zip(scores, kv_refs):
            half = kv.shape[0] // 2
            p = jnp.exp2(s * scale - wide(top, half))
            values = kv[half:, :]
            values = jnp.concatenate([values, jnp.ones_like(values)], axis=1)
            part = jnp.dot(p.astype(jnp.bfloat16), values, preferred_element_type=jnp.float32)
            acc = part if acc is None else acc + part
        if final:
            outs[0][here, :] = (acc[:, :head_dim] / acc[:, head_dim:]).astype(jnp.bfloat16)
        else:
            outs[0][here, :] = top
            outs[1][here, :] = acc
        return 0

    lax.fori_loop(0, rows // TILE, body, 0, unroll=min(UNROLL, rows // TILE))


def attend(order, queries, state, pieces, final, group, scale, span=None):
    span = span or (0, queries.shape[0])
    rows, head_dim = span[1], queries.shape[1]
    masks = tuple(mask for mask, _ in pieces)
    keys = sum(piece.shape[0] // 2 for _, piece in pieces)
    if final:
        shapes = [jax.ShapeDtypeStruct((rows, head_dim), jnp.bfloat16)]
    else:
        shapes = [
            jax.ShapeDtypeStruct((rows, head_dim), jnp.float32),
            jax.ShapeDtypeStruct((rows, 2 * head_dim), jnp.float32),
        ]
    operands = [queries, *(state or []), *(piece for _, piece in pieces)]
    table = [] if set(masks) == {None} else [order]
    return pl.pallas_call(
        functools.partial(attend_kernel, span, masks, state is not None, final, group, scale),
        out_shape=shapes,
        in_specs=[SMEM] * len(table) + [VMEM] * len(operands),
        out_specs=[VMEM] * len(shapes),
        compiler_params=pltpu.CompilerParams(vmem_limit_bytes=LIMIT),
        cost_estimate=pl.CostEstimate(
            flops=6 * rows * keys * head_dim,
            bytes_accessed=rows * head_dim * 4,
            transcendentals=rows * keys,
        ),
        name="attend",
    )(*table, *operands)


def butterfly(value, axis, size, keep_last=False):
    step = 1
    pair = None
    while step < size:
        if pair is not None:
            value = pair[0] + pair[1]
        pair = (value, lax.ppermute(value, axis, [(i, i ^ step) for i in range(size)]))
        step *= 2
    return pair if keep_last else pair[0] + pair[1]


def gather_blocks(value, count, before=None):
    held = {0: value}
    step = count // 2
    while step:
        perm = [(i, i ^ step) for i in range(count)]
        for mask in list(held):
            sent = held[mask]
            if before is not None and (mask ^ step) == count - 1:
                sent, before = lax.optimization_barrier((sent, before))
            held[mask ^ step] = lax.ppermute(sent, "blk", perm)
        step //= 2
    return held, before


def on_device(
    queries,
    features,
    adapter_down,
    adapter_key_up,
    adapter_value_up,
    base_key,
    base_value,
    prefix_key,
    prefix_value,
    adapter_ids,
    block_order,
):
    block_count = lax.axis_size("blk")
    team_count = lax.axis_size("team")
    query_dev, kv_heads, group_dev, head_dim = queries.shape
    mine = lax.axis_index("team") & 1
    scale = LOG2E / math.sqrt(head_dim)
    rows = query_dev * group_dev

    def swap(value):
        return lax.ppermute(value, "team", [(i, i ^ 1) for i in range(team_count)])

    def pick(array, axis, other=False):
        index = 1 - mine if other else mine
        return lax.dynamic_index_in_dim(array, index, axis, keepdims=False)

    latent = partial_latent(adapter_ids, block_order, features, jnp.swapaxes(adapter_down, 1, 2))
    own_prefix = jnp.concatenate([pick(prefix_key, 1), pick(prefix_value, 1)], axis=0)
    latent, own_prefix = lax.optimization_barrier((latent, own_prefix))
    latent = butterfly(latent, "head", lax.axis_size("head"))
    first, second = butterfly(latent, "team", team_count, True)

    prefix, _ = gather_blocks(own_prefix, block_count)
    own_queries = pick(queries, 1).reshape(rows, head_dim)
    far_queries = swap(pick(queries, 1, True).reshape(rows, head_dim))
    own_new = expand(
        adapter_ids,
        first,
        second,
        pick(adapter_key_up, 2),
        pick(adapter_value_up, 2),
        pick(base_key, 1),
        pick(base_value, 1),
    )
    last = block_count - 1
    early = [(None, piece) for mask, piece in prefix.items() if mask != last]
    far_state = attend(block_order, far_queries, None, early, False, group_dev, scale)
    new, far_state = gather_blocks(own_new, block_count, far_state)
    own_state = attend(block_order, own_queries, None, early, False, group_dev, scale)
    far_state, own_state = lax.optimization_barrier((far_state, own_state))
    late = [(None, prefix[last])] + list(new.items())
    parts = 2 if rows % (2 * TILE) == 0 else 1
    part = rows // parts
    received = []
    for n in range(parts):
        span = (n * part, part)
        out = attend(block_order, far_queries, far_state, late, True, group_dev, scale, span)[0]
        received.append(swap(out))
    own_out = attend(block_order, own_queries, own_state, late, True, group_dev, scale)[0]
    shape = (query_dev, 1, group_dev, head_dim)
    head = lax.broadcasted_iota(jnp.int32, queries.shape, 1)
    received = jnp.concatenate(received, axis=0)
    return jnp.where(head == mine, own_out.reshape(shape), received.reshape(shape))


def solution(mesh):
    placed = (
        P("blk", "head", "team", None),
        P("blk", ("team", "head")),
        P(None, ("team", "head"), None),
        P(None, None, "head", None),
        P(None, None, "head", None),
        P("blk", "head", None),
        P("blk", "head", None),
        P("blk", "head", None),
        P("blk", "head", None),
        P(),
        P(),
    )
    return jax.shard_map(
        on_device,
        mesh=mesh,
        in_specs=placed,
        out_specs=P("blk", "head", "team", None),
        check_vma=False,
    )
```

```python
import functools
import math

import jax
import jax.numpy as jnp
from jax import lax
from jax.experimental import pallas as pl
from jax.experimental.pallas import tpu as pltpu
from jax.sharding import PartitionSpec as P


NEG_FILL = -1e30
LOG2E = 1.4426950408889634
TILE = 128
UNROLL = 8
LIMIT = 20 * 2**20
VMEM = pl.BlockSpec(memory_space=pltpu.VMEM)
SMEM = pl.BlockSpec(memory_space=pltpu.SMEM)


def dot_t(a, b):
    return lax.dot_general(a, b, (((1,), (1,)), ((), ())), preferred_element_type=jnp.float32)


def latent_kernel(ids_ref, order_ref, features_ref, down_ref, out_ref, bound_ref, held, sem):
    me = lax.axis_index("blk")
    copy = pltpu.make_async_copy(down_ref.at[ids_ref[me]], held, sem)
    copy.start()
    tokens = features_ref.shape[0]
    for mask in range(order_ref.shape[0]):
        bound = (order_ref[me] - order_ref[me ^ mask]) * tokens
        bound_ref[mask : mask + 1, :] = jnp.full((1, bound_ref.shape[1]), bound, jnp.int32)
    copy.wait()
    out_ref[...] = dot_t(held[...], features_ref[...])


def partial_latent(ids, order, features, down):
    tokens, depth = features.shape
    rank = down.shape[1]
    return pl.pallas_call(
        latent_kernel,
        out_shape=[
            jax.ShapeDtypeStruct((rank, tokens), jnp.float32),
            jax.ShapeDtypeStruct((order.shape[0], 128), jnp.int32),
        ],
        in_specs=[SMEM, SMEM, VMEM, pl.BlockSpec(memory_space=pl.ANY)],
        out_specs=[VMEM, VMEM],
        scratch_shapes=[pltpu.VMEM((rank, depth), down.dtype), pltpu.SemaphoreType.DMA(())],
        compiler_params=pltpu.CompilerParams(vmem_limit_bytes=LIMIT),
        cost_estimate=pl.CostEstimate(
            flops=2 * tokens * depth * rank,
            bytes_accessed=2 * depth * (tokens + rank),
            transcendentals=0,
        ),
        name="partial_latent",
    )(ids, order, features, down)


def expand_kernel(ids_ref, first, second, key_up, value_up, key_base, value_base, out_ref):
    chosen = ids_ref[lax.axis_index("blk")]
    latent = (first[...] + second[...]).astype(jnp.bfloat16)
    tokens = key_base.shape[0]
    for n, (up, base) in enumerate(((key_up, key_base), (value_up, value_base))):
        delta = lax.dot_general(
            latent, up[chosen], (((0,), (0,)), ((), ())), preferred_element_type=jnp.float32
        )
        out_ref[n * tokens : (n + 1) * tokens, :] = (
            base[...].astype(jnp.float32) + delta
        ).astype(jnp.bfloat16)


def expand(ids, first, second, key_up, value_up, key_base, value_base):
    tokens, head_dim = key_base.shape
    return pl.pallas_call(
        expand_kernel,
        out_shape=jax.ShapeDtypeStruct((2 * tokens, head_dim), jnp.bfloat16),
        in_specs=[SMEM] + [VMEM] * 6,
        out_specs=VMEM,
        compiler_params=pltpu.CompilerParams(vmem_limit_bytes=LIMIT),
        cost_estimate=pl.CostEstimate(
            flops=4 * tokens * head_dim * first.shape[0],
            bytes_accessed=8 * tokens * head_dim,
            transcendentals=0,
        ),
        name="expand",
    )(ids, first, second, key_up, value_up, key_base, value_base)


def wide(value, width):
    return jnp.concatenate([value] * (width // value.shape[1]), axis=1)


def attend_kernel(span, masks, carried, final, group, scale, *refs):
    bound_ref, refs = (None, refs) if set(masks) == {None} else (refs[0], refs[1:])
    q_ref, refs = refs[0], refs[1:]
    state_refs, refs = refs[: 2 * carried], refs[2 * carried :]
    kv_refs, outs = refs[: len(masks)], refs[len(masks) :]
    head_dim = q_ref.shape[1]
    start, rows = span

    def body(i, _):
        here = pl.ds(pl.multiple_of(i * TILE, TILE), TILE)
        at = pl.ds(pl.multiple_of(start + i * TILE, TILE), TILE)
        q = q_ref[at, :]
        scores = []
        top = None
        for kv, mask in zip(kv_refs, masks):
            half = kv.shape[0] // 2
            s = dot_t(q, kv[:half, :])
            if mask is not None:
                limit = bound_ref[mask : mask + 1, :] * group + (start + i * TILE)
                ahead = lax.broadcasted_iota(jnp.int32, (TILE, half), 1) * group
                ahead = ahead - lax.broadcasted_iota(jnp.int32, (TILE, half), 0)
                s = jnp.where(ahead <= wide(limit, half), s, NEG_FILL)
            scores.append(s)
            most = jnp.max(s, axis=1, keepdims=True)
            top = most if top is None else jnp.maximum(top, most)
        top = jnp.broadcast_to(top * scale, (TILE, head_dim))
        acc = None
        if carried:
            old = state_refs[0][at, :]
            top = jnp.maximum(top, old)
            acc = state_refs[1][at, :] * wide(jnp.exp2(old - top), 2 * head_dim)
        for s, kv in zip(scores, kv_refs):
            half = kv.shape[0] // 2
            p = jnp.exp2(s * scale - wide(top, half))
            values = kv[half:, :]
            values = jnp.concatenate([values, jnp.ones_like(values)], axis=1)
            part = jnp.dot(p.astype(jnp.bfloat16), values, preferred_element_type=jnp.float32)
            acc = part if acc is None else acc + part
        if final:
            outs[0][here, :] = (acc[:, :head_dim] / acc[:, head_dim:]).astype(jnp.bfloat16)
        else:
            outs[0][here, :] = top
            outs[1][here, :] = acc
        return 0

    lax.fori_loop(0, rows // TILE, body, 0, unroll=min(UNROLL, rows // TILE))


def attend(bounds, queries, state, pieces, final, group, scale, span=None):
    span = span or (0, queries.shape[0])
    rows, head_dim = span[1], queries.shape[1]
    masks = tuple(mask for mask, _ in pieces)
    keys = sum(piece.shape[0] // 2 for _, piece in pieces)
    if final:
        shapes = [jax.ShapeDtypeStruct((rows, head_dim), jnp.bfloat16)]
    else:
        shapes = [
            jax.ShapeDtypeStruct((rows, head_dim), jnp.float32),
            jax.ShapeDtypeStruct((rows, 2 * head_dim), jnp.float32),
        ]
    operands = [queries, *(state or []), *(piece for _, piece in pieces)]
    table = [] if set(masks) == {None} else [bounds]
    return pl.pallas_call(
        functools.partial(attend_kernel, span, masks, state is not None, final, group, scale),
        out_shape=shapes,
        in_specs=[VMEM] * len(table + operands),
        out_specs=[VMEM] * len(shapes),
        compiler_params=pltpu.CompilerParams(vmem_limit_bytes=LIMIT),
        cost_estimate=pl.CostEstimate(
            flops=6 * rows * keys * head_dim,
            bytes_accessed=rows * head_dim * 4,
            transcendentals=rows * keys,
        ),
        name="attend",
    )(*table, *operands)


def butterfly(value, axis, size):
    step = 1
    pair = (value, None)
    while step < size:
        value = pair[0] if pair[1] is None else pair[0] + pair[1]
        pair = (value, lax.ppermute(value, axis, [(i, i ^ step) for i in range(size)]))
        step *= 2
    return pair


def gather_blocks(value, count, before=None):
    held = {0: value}
    step = count // 2
    while step:
        perm = [(i, i ^ step) for i in range(count)]
        for mask in list(held):
            sent = held[mask]
            if before is not None and (mask ^ step) == count - 1:
                sent, before = lax.optimization_barrier((sent, before))
            held[mask ^ step] = lax.ppermute(sent, "blk", perm)
        step //= 2
    return held, before


def on_device(
    queries,
    features,
    adapter_down,
    adapter_key_up,
    adapter_value_up,
    base_key,
    base_value,
    prefix_key,
    prefix_value,
    adapter_ids,
    block_order,
):
    block_count = lax.axis_size("blk")
    team_count = lax.axis_size("team")
    query_dev, _, group_dev, head_dim = queries.shape
    mine = lax.axis_index("team") & 1
    scale = LOG2E / math.sqrt(head_dim)
    rows = query_dev * group_dev

    def swap(value):
        return lax.ppermute(value, "team", [(i, i ^ 1) for i in range(team_count)])

    def pick(array, axis, other=False):
        index = 1 - mine if other else mine
        return lax.dynamic_index_in_dim(array, index, axis, keepdims=False)

    latent, bounds = partial_latent(adapter_ids, block_order, features, jnp.swapaxes(adapter_down, 1, 2))
    own_prefix = pick(jnp.concatenate([prefix_key, prefix_value], axis=0), 1)
    first, second = butterfly(latent, "head", lax.axis_size("head"))
    first, second = butterfly(first + second, "team", team_count)

    prefix, _ = gather_blocks(own_prefix, block_count)
    own_queries = pick(queries, 1).reshape(rows, head_dim)
    far_queries = swap(pick(queries, 1, True).reshape(rows, head_dim))
    own_new = expand(
        adapter_ids,
        first,
        second,
        pick(adapter_key_up, 2),
        pick(adapter_value_up, 2),
        pick(base_key, 1),
        pick(base_value, 1),
    )
    last = block_count - 1
    early = [(None, piece) for mask, piece in prefix.items() if mask != last]
    own_state = attend(bounds, own_queries, None, early, False, group_dev, scale)
    new, own_state = gather_blocks(own_new, block_count, own_state)
    far_state = attend(bounds, far_queries, None, early, False, group_dev, scale)
    middle = [(mask, new[mask]) for mask in new if mask in (0, block_count // 2)]
    tail = [(None, prefix[last])]
    tail += [(mask, new[mask]) for mask in new if mask not in (0, block_count // 2)]
    far_state = attend(bounds, far_queries, far_state, middle, False, group_dev, scale)
    own_state = attend(bounds, own_queries, own_state, middle, False, group_dev, scale)
    far_state, own_state = lax.optimization_barrier((far_state, own_state))
    parts = 2 if rows % (2 * TILE) == 0 else 1
    part = rows // parts
    received = []
    for n in range(parts):
        span = (n * part, part)
        out = attend(bounds, far_queries, far_state, tail, True, group_dev, scale, span)[0]
        received.append(swap(out))
    own_out = attend(bounds, own_queries, own_state, tail, True, group_dev, scale)[0]
    shape = (query_dev, 1, group_dev, head_dim)
    head = lax.broadcasted_iota(jnp.int32, queries.shape, 1)
    received = jnp.concatenate(received, axis=0)
    return jnp.where(head == mine, own_out.reshape(shape), received.reshape(shape))


def solution(mesh):
    placed = (
        P("blk", "head", "team", None),
        P("blk", ("team", "head")),
        P(None, ("team", "head"), None),
        P(None, None, "head", None),
        P(None, None, "head", None),
        P("blk", "head", None),
        P("blk", "head", None),
        P("blk", "head", None),
        P("blk", "head", None),
        P(),
        P(),
    )

    return jax.shard_map(
        on_device,
        mesh=mesh,
        in_specs=placed,
        out_specs=P("blk", "head", "team", None),
        check_vma=False,
    )
```

```python
import functools
import math

import jax
import jax.numpy as jnp
from jax import lax
from jax.experimental import pallas as pl
from jax.experimental.pallas import tpu as pltpu
from jax.sharding import PartitionSpec as P


NEG_FILL = -1e30
LOG2E = 1.4426950408889634
TILE = 128
UNROLL = 8
LIMIT = 20 * 2**20
VMEM = pl.BlockSpec(memory_space=pltpu.VMEM)
SMEM = pl.BlockSpec(memory_space=pltpu.SMEM)


def dot_t(a, b):
    return lax.dot_general(a, b, (((1,), (1,)), ((), ())), preferred_element_type=jnp.float32)


def latent_kernel(ids_ref, order_ref, features_ref, down_ref, out_ref, bound_ref, held, sem):
    me = lax.axis_index("blk")
    copy = pltpu.make_async_copy(down_ref.at[ids_ref[me]], held, sem)
    copy.start()
    tokens = features_ref.shape[0]
    for mask in range(order_ref.shape[0]):
        bound = (order_ref[me] - order_ref[me ^ mask]) * tokens
        bound_ref[mask : mask + 1, :] = jnp.full((1, bound_ref.shape[1]), bound, jnp.int32)
    copy.wait()
    out_ref[...] = dot_t(held[...], features_ref[...])


def partial_latent(ids, order, features, down):
    tokens, depth = features.shape
    rank = down.shape[1]
    return pl.pallas_call(
        latent_kernel,
        out_shape=[
            jax.ShapeDtypeStruct((rank, tokens), jnp.float32),
            jax.ShapeDtypeStruct((order.shape[0], 128), jnp.int32),
        ],
        in_specs=[SMEM, SMEM, VMEM, pl.BlockSpec(memory_space=pl.ANY)],
        out_specs=[VMEM, VMEM],
        scratch_shapes=[pltpu.VMEM((rank, depth), down.dtype), pltpu.SemaphoreType.DMA(())],
        compiler_params=pltpu.CompilerParams(vmem_limit_bytes=LIMIT),
        cost_estimate=pl.CostEstimate(
            flops=2 * tokens * depth * rank,
            bytes_accessed=2 * depth * (tokens + rank),
            transcendentals=0,
        ),
        name="partial_latent",
    )(ids, order, features, down)


def expand_kernel(ids_ref, first, second, key_up, value_up, key_base, value_base, out_ref):
    chosen = ids_ref[lax.axis_index("blk")]
    latent = (first[...] + second[...].astype(jnp.float32)).astype(jnp.bfloat16)
    tokens = key_base.shape[0]
    for n, (up, base) in enumerate(((key_up, key_base), (value_up, value_base))):
        delta = lax.dot_general(
            latent, up[chosen], (((0,), (0,)), ((), ())), preferred_element_type=jnp.float32
        )
        out_ref[n * tokens : (n + 1) * tokens, :] = (
            base[...].astype(jnp.float32) + delta
        ).astype(jnp.bfloat16)


def expand(ids, first, second, key_up, value_up, key_base, value_base):
    tokens, head_dim = key_base.shape
    return pl.pallas_call(
        expand_kernel,
        out_shape=jax.ShapeDtypeStruct((2 * tokens, head_dim), jnp.bfloat16),
        in_specs=[SMEM] + [VMEM] * 6,
        out_specs=VMEM,
        compiler_params=pltpu.CompilerParams(vmem_limit_bytes=LIMIT),
        cost_estimate=pl.CostEstimate(
            flops=4 * tokens * head_dim * first.shape[0],
            bytes_accessed=8 * tokens * head_dim,
            transcendentals=0,
        ),
        name="expand",
    )(ids, first, second, key_up, value_up, key_base, value_base)


def wide(value, width):
    return jnp.concatenate([value] * (width // value.shape[1]), axis=1)


def attend_kernel(span, masks, carried, final, group, scale, *refs):
    bound_ref, refs = (None, refs) if set(masks) == {None} else (refs[0], refs[1:])
    q_ref, refs = refs[0], refs[1:]
    state_refs, refs = refs[: 2 * carried], refs[2 * carried :]
    kv_refs, outs = refs[: len(masks)], refs[len(masks) :]
    head_dim = q_ref.shape[1]
    start, rows = span

    def body(i, _):
        here = pl.ds(pl.multiple_of(i * TILE, TILE), TILE)
        at = pl.ds(pl.multiple_of(start + i * TILE, TILE), TILE)
        q = q_ref[at, :]
        scores = []
        top = None
        for kv, mask in zip(kv_refs, masks):
            half = kv.shape[0] // 2
            s = dot_t(q, kv[:half, :])
            if mask is not None:
                limit = bound_ref[mask : mask + 1, :] * group + (start + i * TILE)
                ahead = lax.broadcasted_iota(jnp.int32, (TILE, half), 1) * group
                ahead = ahead - lax.broadcasted_iota(jnp.int32, (TILE, half), 0)
                s = jnp.where(ahead <= wide(limit, half), s, NEG_FILL)
            scores.append(s)
            most = jnp.max(s, axis=1, keepdims=True)
            top = most if top is None else jnp.maximum(top, most)
        top = jnp.broadcast_to(top * scale, (TILE, head_dim))
        acc = None
        if carried:
            old = state_refs[0][at, :]
            top = jnp.maximum(top, old)
            acc = state_refs[1][at, :] * wide(jnp.exp2(old - top), 2 * head_dim)
        for s, kv in zip(scores, kv_refs):
            half = kv.shape[0] // 2
            p = jnp.exp2(s * scale - wide(top, half))
            values = kv[half:, :]
            values = jnp.concatenate([values, jnp.ones_like(values)], axis=1)
            part = jnp.dot(p.astype(jnp.bfloat16), values, preferred_element_type=jnp.float32)
            acc = part if acc is None else acc + part
        if final:
            outs[0][here, :] = (acc[:, :head_dim] / acc[:, head_dim:]).astype(jnp.bfloat16)
        else:
            outs[0][here, :] = top
            outs[1][here, :] = acc
        return 0

    lax.fori_loop(0, rows // TILE, body, 0, unroll=min(UNROLL, rows // TILE))


def attend(bounds, queries, state, pieces, final, group, scale, span=None):
    span = span or (0, queries.shape[0])
    rows, head_dim = span[1], queries.shape[1]
    masks = tuple(mask for mask, _ in pieces)
    keys = sum(piece.shape[0] // 2 for _, piece in pieces)
    if final:
        shapes = [jax.ShapeDtypeStruct((rows, head_dim), jnp.bfloat16)]
    else:
        shapes = [
            jax.ShapeDtypeStruct((rows, head_dim), jnp.float32),
            jax.ShapeDtypeStruct((rows, 2 * head_dim), jnp.float32),
        ]
    operands = [queries, *(state or []), *(piece for _, piece in pieces)]
    table = [] if set(masks) == {None} else [bounds]
    return pl.pallas_call(
        functools.partial(attend_kernel, span, masks, state is not None, final, group, scale),
        out_shape=shapes,
        in_specs=[VMEM] * len(table + operands),
        out_specs=[VMEM] * len(shapes),
        compiler_params=pltpu.CompilerParams(vmem_limit_bytes=LIMIT),
        cost_estimate=pl.CostEstimate(
            flops=6 * rows * keys * head_dim,
            bytes_accessed=rows * head_dim * 4,
            transcendentals=rows * keys,
        ),
        name="attend",
    )(*table, *operands)


def butterfly(value, axis, size):
    step = 1
    pair = (value, None)
    while step < size:
        value = pair[0] if pair[1] is None else pair[0] + pair[1].astype(jnp.float32)
        perm = [(i, i ^ step) for i in range(size)]
        pair = (value, lax.ppermute(value.astype(jnp.bfloat16), axis, perm))
        step *= 2
    return pair


def gather_blocks(value, count, before=None):
    held = {0: value}
    step = count // 2
    while step:
        perm = [(i, i ^ step) for i in range(count)]
        for mask in list(held):
            sent = held[mask]
            if before is not None and (mask ^ step) == count - 1:
                sent, before = lax.optimization_barrier((sent, before))
            held[mask ^ step] = lax.ppermute(sent, "blk", perm)
        step //= 2
    return held, before


def on_device(
    queries,
    features,
    adapter_down,
    adapter_key_up,
    adapter_value_up,
    base_key,
    base_value,
    prefix_key,
    prefix_value,
    adapter_ids,
    block_order,
):
    block_count = lax.axis_size("blk")
    team_count = lax.axis_size("team")
    query_dev, _, group_dev, head_dim = queries.shape
    mine = lax.axis_index("team") & 1
    scale = LOG2E / math.sqrt(head_dim)
    rows = query_dev * group_dev

    def swap(value):
        return lax.ppermute(value, "team", [(i, i ^ 1) for i in range(team_count)])

    def pick(array, axis, other=False):
        index = 1 - mine if other else mine
        return lax.dynamic_index_in_dim(array, index, axis, keepdims=False)

    latent, bounds = partial_latent(adapter_ids, block_order, features, jnp.swapaxes(adapter_down, 1, 2))
    own_prefix = pick(jnp.concatenate([prefix_key, prefix_value], axis=0), 1)
    first, second = butterfly(latent, "head", lax.axis_size("head"))
    first, second = butterfly(first + second.astype(jnp.float32), "team", team_count)

    prefix, _ = gather_blocks(own_prefix, block_count)
    own_queries = pick(queries, 1).reshape(rows, head_dim)
    far_queries = swap(pick(queries, 1, True).reshape(rows, head_dim))
    own_new = expand(
        adapter_ids,
        first,
        second,
        pick(adapter_key_up, 2),
        pick(adapter_value_up, 2),
        pick(base_key, 1),
        pick(base_value, 1),
    )
    last = block_count - 1
    early = [(None, piece) for mask, piece in prefix.items() if mask != last]
    own_state = attend(bounds, own_queries, None, early, False, group_dev, scale)
    new, own_state = gather_blocks(own_new, block_count, own_state)
    far_state = attend(bounds, far_queries, None, early, False, group_dev, scale)
    half = block_count // 2
    relayed = [(None, prefix[last])]
    middle = [(mask, new[mask]) for mask in new if mask in (0, half)]
    tail = [(mask, new[mask]) for mask in new if mask not in (0, half)]
    own_state = attend(bounds, own_queries, own_state, middle, False, group_dev, scale)
    far_state = attend(bounds, far_queries, far_state, middle + relayed, False, group_dev, scale)
    far_state, own_state = lax.optimization_barrier((far_state, own_state))
    parts = 2 if rows % (2 * TILE) == 0 else 1
    part = rows // parts
    received = []
    for n in range(parts):
        span = (n * part, part)
        out = attend(bounds, far_queries, far_state, tail, True, group_dev, scale, span)[0]
        received.append(swap(out))
    own_out = attend(bounds, own_queries, own_state, relayed + tail, True, group_dev, scale)[0]
    shape = (query_dev, 1, group_dev, head_dim)
    head = lax.broadcasted_iota(jnp.int32, queries.shape, 1)
    received = jnp.concatenate(received, axis=0)
    return jnp.where(head == mine, own_out.reshape(shape), received.reshape(shape))


def solution(mesh):
    placed = (
        P("blk", "head", "team", None),
        P("blk", ("team", "head")),
        P(None, ("team", "head"), None),
        P(None, None, "head", None),
        P(None, None, "head", None),
        P("blk", "head", None),
        P("blk", "head", None),
        P("blk", "head", None),
        P("blk", "head", None),
        P(),
        P(),
    )

    return jax.shard_map(
        on_device,
        mesh=mesh,
        in_specs=placed,
        out_specs=P("blk", "head", "team", None),
        check_vma=False,
    )
```

```python
import functools
import math

import jax
import jax.numpy as jnp
from jax import lax
from jax.experimental import pallas as pl
from jax.experimental.pallas import tpu as pltpu
from jax.sharding import PartitionSpec as P


NEG_FILL = -1e30
LOG2E = 1.4426950408889634
TILE = 128
UNROLL = 8
LIMIT = 20 * 2**20
VMEM = pl.BlockSpec(memory_space=pltpu.VMEM)
SMEM = pl.BlockSpec(memory_space=pltpu.SMEM)


def dot_t(a, b):
    return lax.dot_general(a, b, (((1,), (1,)), ((), ())), preferred_element_type=jnp.float32)


def latent_kernel(ids_ref, order_ref, features_ref, down_ref, out_ref, bound_ref, held, sem):
    me = lax.axis_index("blk")
    copy = pltpu.make_async_copy(down_ref.at[ids_ref[me]], held, sem)
    copy.start()
    tokens = features_ref.shape[0]
    for mask in range(order_ref.shape[0]):
        bound = (order_ref[me] - order_ref[me ^ mask]) * tokens
        bound_ref[mask : mask + 1, :] = jnp.full((1, bound_ref.shape[1]), bound, jnp.int32)
    copy.wait()
    out_ref[...] = dot_t(held[...], features_ref[...])


def partial_latent(ids, order, features, down):
    tokens, depth = features.shape
    rank = down.shape[1]
    return pl.pallas_call(
        latent_kernel,
        out_shape=[
            jax.ShapeDtypeStruct((rank, tokens), jnp.float32),
            jax.ShapeDtypeStruct((order.shape[0], 128), jnp.int32),
        ],
        in_specs=[SMEM, SMEM, VMEM, pl.BlockSpec(memory_space=pl.ANY)],
        out_specs=[VMEM, VMEM],
        scratch_shapes=[pltpu.VMEM((rank, depth), down.dtype), pltpu.SemaphoreType.DMA(())],
        compiler_params=pltpu.CompilerParams(vmem_limit_bytes=LIMIT),
        cost_estimate=pl.CostEstimate(
            flops=2 * tokens * depth * rank,
            bytes_accessed=2 * depth * (tokens + rank),
            transcendentals=0,
        ),
        name="partial_latent",
    )(ids, order, features, down)


def expand_kernel(ids_ref, first, second, key_up, value_up, key_base, value_base, out_ref):
    chosen = ids_ref[lax.axis_index("blk")]
    latent = (first[...] + second[...]).astype(jnp.bfloat16)
    tokens = key_base.shape[0]
    for n, (up, base) in enumerate(((key_up, key_base), (value_up, value_base))):
        delta = lax.dot_general(
            latent, up[chosen], (((0,), (0,)), ((), ())), preferred_element_type=jnp.float32
        )
        out_ref[n * tokens : (n + 1) * tokens, :] = (
            base[...].astype(jnp.float32) + delta
        ).astype(jnp.bfloat16)


def expand(ids, first, second, key_up, value_up, key_base, value_base):
    tokens, head_dim = key_base.shape
    return pl.pallas_call(
        expand_kernel,
        out_shape=jax.ShapeDtypeStruct((2 * tokens, head_dim), jnp.bfloat16),
        in_specs=[SMEM] + [VMEM] * 6,
        out_specs=VMEM,
        compiler_params=pltpu.CompilerParams(vmem_limit_bytes=LIMIT),
        cost_estimate=pl.CostEstimate(
            flops=4 * tokens * head_dim * first.shape[0],
            bytes_accessed=8 * tokens * head_dim,
            transcendentals=0,
        ),
        name="expand",
    )(ids, first, second, key_up, value_up, key_base, value_base)


def wide(value, width):
    return jnp.concatenate([value] * (width // value.shape[1]), axis=1)


def attend_kernel(span, masks, carried, final, group, scale, *refs):
    bound_ref, refs = (None, refs) if set(masks) == {None} else (refs[0], refs[1:])
    q_ref, refs = refs[0], refs[1:]
    state_refs, refs = refs[: 2 * carried], refs[2 * carried :]
    kv_refs, outs = refs[: len(masks)], refs[len(masks) :]
    head_dim = q_ref.shape[1]
    start, rows = span

    def body(i, _):
        here = pl.ds(pl.multiple_of(i * TILE, TILE), TILE)
        at = pl.ds(pl.multiple_of(start + i * TILE, TILE), TILE)
        q = q_ref[at, :]
        scores = []
        top = None
        for kv, mask in zip(kv_refs, masks):
            half = kv.shape[0] // 2
            s = dot_t(q, kv[:half, :])
            if mask is not None:
                limit = bound_ref[mask : mask + 1, :] * group + (start + i * TILE)
                ahead = lax.broadcasted_iota(jnp.int32, (TILE, half), 1) * group
                ahead = ahead - lax.broadcasted_iota(jnp.int32, (TILE, half), 0)
                s = jnp.where(ahead <= wide(limit, half), s, NEG_FILL)
            scores.append(s)
            most = jnp.max(s, axis=1, keepdims=True)
            top = most if top is None else jnp.maximum(top, most)
        top = jnp.broadcast_to(top * scale, (TILE, head_dim))
        acc = None
        if carried:
            old = state_refs[0][at, :]
            top = jnp.maximum(top, old)
            acc = state_refs[1][at, :] * wide(jnp.exp2(old - top), 2 * head_dim)
        for s, kv in zip(scores, kv_refs):
            half = kv.shape[0] // 2
            p = jnp.exp2(s * scale - wide(top, half))
            values = kv[half:, :]
            values = jnp.concatenate([values, jnp.ones_like(values)], axis=1)
            part = jnp.dot(p.astype(jnp.bfloat16), values, preferred_element_type=jnp.float32)
            acc = part if acc is None else acc + part
        if final:
            outs[0][here, :] = (acc[:, :head_dim] / acc[:, head_dim:]).astype(jnp.bfloat16)
        else:
            outs[0][here, :] = top
            outs[1][here, :] = acc
        return 0

    lax.fori_loop(0, rows // TILE, body, 0, unroll=min(UNROLL, rows // TILE))


def attend(bounds, queries, state, pieces, final, group, scale, span=None):
    span = span or (0, queries.shape[0])
    rows, head_dim = span[1], queries.shape[1]
    masks = tuple(mask for mask, _ in pieces)
    keys = sum(piece.shape[0] // 2 for _, piece in pieces)
    if final:
        shapes = [jax.ShapeDtypeStruct((rows, head_dim), jnp.bfloat16)]
    else:
        shapes = [
            jax.ShapeDtypeStruct((rows, head_dim), jnp.float32),
            jax.ShapeDtypeStruct((rows, 2 * head_dim), jnp.float32),
        ]
    operands = [queries, *(state or []), *(piece for _, piece in pieces)]
    table = [] if set(masks) == {None} else [bounds]
    return pl.pallas_call(
        functools.partial(attend_kernel, span, masks, state is not None, final, group, scale),
        out_shape=shapes,
        in_specs=[VMEM] * len(table + operands),
        out_specs=[VMEM] * len(shapes),
        compiler_params=pltpu.CompilerParams(vmem_limit_bytes=LIMIT),
        cost_estimate=pl.CostEstimate(
            flops=6 * rows * keys * head_dim,
            bytes_accessed=rows * head_dim * 4,
            transcendentals=rows * keys,
        ),
        name="attend",
    )(*table, *operands)


def butterfly(value, axis, size):
    step = 1
    pair = (value, None)
    while step < size:
        value = pair[0] if pair[1] is None else pair[0] + pair[1]
        perm = [(i, i ^ step) for i in range(size)]
        pair = (value, lax.ppermute(value, axis, perm))
        step *= 2
    return pair


def gather_blocks(value, count, before=None):
    held = {0: value}
    step = count // 2
    while step:
        perm = [(i, i ^ step) for i in range(count)]
        for mask in list(held):
            sent = held[mask]
            if before is not None and (mask ^ step) == count - 1:
                sent, before = lax.optimization_barrier((sent, before))
            held[mask ^ step] = lax.ppermute(sent, "blk", perm)
        step //= 2
    return held, before


def on_device(
    queries,
    features,
    adapter_down,
    adapter_key_up,
    adapter_value_up,
    base_key,
    base_value,
    prefix_key,
    prefix_value,
    adapter_ids,
    block_order,
):
    block_count = lax.axis_size("blk")
    team_count = lax.axis_size("team")
    query_dev, _, group_dev, head_dim = queries.shape
    mine = lax.axis_index("team") & 1
    scale = LOG2E / math.sqrt(head_dim)
    rows = query_dev * group_dev

    def swap(value):
        return lax.ppermute(value, "team", [(i, i ^ 1) for i in range(team_count)])

    def pick(array, axis, other=False):
        index = 1 - mine if other else mine
        return lax.dynamic_index_in_dim(array, index, axis, keepdims=False)

    latent, bounds = partial_latent(adapter_ids, block_order, features, jnp.swapaxes(adapter_down, 1, 2))
    own_prefix = pick(jnp.concatenate([prefix_key, prefix_value], axis=0), 1)
    first, second = butterfly(latent, "head", lax.axis_size("head"))
    first, second = butterfly(first + second, "team", team_count)

    prefix, _ = gather_blocks(own_prefix, block_count)
    own_queries = pick(queries, 1).reshape(rows, head_dim)
    far_queries = swap(pick(queries, 1, True).reshape(rows, head_dim))
    own_new = expand(
        adapter_ids,
        first,
        second,
        pick(adapter_key_up, 2),
        pick(adapter_value_up, 2),
        pick(base_key, 1),
        pick(base_value, 1),
    )
    last = block_count - 1
    early = [(None, piece) for mask, piece in prefix.items() if mask != last]
    own_state = attend(bounds, own_queries, None, early, False, group_dev, scale)
    new, own_state = gather_blocks(own_new, block_count, own_state)
    far_state = attend(bounds, far_queries, None, early, False, group_dev, scale)
    half = block_count // 2
    relayed = [(None, prefix[last])]
    middle = [(mask, new[mask]) for mask in new if mask in (0, half)]
    tail = [(mask, new[mask]) for mask in new if mask not in (0, half)]
    own_state = attend(bounds, own_queries, own_state, middle, False, group_dev, scale)
    far_state = attend(bounds, far_queries, far_state, middle + relayed, False, group_dev, scale)
    far_state, own_state = lax.optimization_barrier((far_state, own_state))
    near = [(mask, piece) for mask, piece in tail if mask != last]
    far_state = attend(bounds, far_queries, far_state, near, False, group_dev, scale)
    parts = 1
    part = rows // parts
    received = []
    for n in range(parts):
        span = (n * part, part)
        out = attend(bounds, far_queries, far_state, tail[-1:], True, group_dev, scale, span)[0]
        received.append(swap(out))
    own_out = attend(bounds, own_queries, own_state, relayed + tail, True, group_dev, scale)[0]
    shape = (query_dev, 1, group_dev, head_dim)
    head = lax.broadcasted_iota(jnp.int32, queries.shape, 1)
    received = jnp.concatenate(received, axis=0)
    return jnp.where(head == mine, own_out.reshape(shape), received.reshape(shape))


def solution(mesh):
    placed = (
        P("blk", "head", "team", None),
        P("blk", ("team", "head")),
        P(None, ("team", "head"), None),
        P(None, None, "head", None),
        P(None, None, "head", None),
        P("blk", "head", None),
        P("blk", "head", None),
        P("blk", "head", None),
        P("blk", "head", None),
        P(),
        P(),
    )

    return jax.shard_map(
        on_device,
        mesh=mesh,
        in_specs=placed,
        out_specs=P("blk", "head", "team", None),
        check_vma=False,
    )
```

```python
import functools
import math

import jax
import jax.numpy as jnp
from jax import lax
from jax.experimental import pallas as pl
from jax.experimental.pallas import tpu as pltpu
from jax.sharding import PartitionSpec as P


NEG_FILL = -1e30
LOG2E = 1.4426950408889634
TILE = 128
UNROLL = 8
LIMIT = 20 * 2**20
VMEM = pl.BlockSpec(memory_space=pltpu.VMEM)
SMEM = pl.BlockSpec(memory_space=pltpu.SMEM)


def dot_t(a, b):
    return lax.dot_general(a, b, (((1,), (1,)), ((), ())), preferred_element_type=jnp.float32)


def latent_kernel(ids_ref, order_ref, features_ref, down_ref, out_ref, bound_ref, chosen_ref):
    me = lax.axis_index("blk")
    chosen = ids_ref[me]
    out_ref[...] = dot_t(down_ref[chosen], features_ref[...])
    tokens = features_ref.shape[0]
    lanes = (1, bound_ref.shape[1])
    for mask in range(order_ref.shape[0]):
        bound = (order_ref[me] - order_ref[me ^ mask]) * tokens
        bound_ref[mask : mask + 1, :] = jnp.full(lanes, bound, jnp.int32)
    for adapter in range(down_ref.shape[0]):
        chosen_ref[adapter : adapter + 1, :] = jnp.full(lanes, chosen - adapter, jnp.int32)


def partial_latent(ids, order, features, down):
    tokens, depth = features.shape
    adapters, rank, _ = down.shape
    return pl.pallas_call(
        latent_kernel,
        out_shape=[
            jax.ShapeDtypeStruct((rank, tokens), jnp.float32),
            jax.ShapeDtypeStruct((order.shape[0], 128), jnp.int32),
            jax.ShapeDtypeStruct((adapters, 128), jnp.int32),
        ],
        in_specs=[SMEM, SMEM, VMEM, VMEM],
        out_specs=[VMEM] * 3,
        compiler_params=pltpu.CompilerParams(vmem_limit_bytes=LIMIT),
        cost_estimate=pl.CostEstimate(
            flops=2 * tokens * depth * rank,
            bytes_accessed=2 * depth * (tokens + rank),
            transcendentals=0,
        ),
        name="partial_latent",
    )(ids, order, features, down)


def expand_kernel(chosen_ref, first, second, key_up, value_up, key_base, value_base, out_ref):
    latent = (first[...] + second[...]).astype(jnp.bfloat16)
    tokens = key_base.shape[0]
    for n, (up, base) in enumerate(((key_up, key_base), (value_up, value_base))):
        delta = None
        for adapter in range(up.shape[0]):
            term = lax.dot_general(
                latent, up[adapter], (((0,), (0,)), ((), ())), preferred_element_type=jnp.float32
            )
            here = chosen_ref[adapter : adapter + 1, : term.shape[1]] == 0
            delta = term if delta is None else jnp.where(here, term, delta)
        out_ref[n * tokens : (n + 1) * tokens, :] = (
            base[...].astype(jnp.float32) + delta
        ).astype(jnp.bfloat16)


def expand(chosen, first, second, key_up, value_up, key_base, value_base):
    tokens, head_dim = key_base.shape
    return pl.pallas_call(
        expand_kernel,
        out_shape=jax.ShapeDtypeStruct((2 * tokens, head_dim), jnp.bfloat16),
        in_specs=[VMEM] * 7,
        out_specs=VMEM,
        compiler_params=pltpu.CompilerParams(vmem_limit_bytes=LIMIT),
        cost_estimate=pl.CostEstimate(
            flops=4 * tokens * head_dim * first.shape[0],
            bytes_accessed=8 * tokens * head_dim,
            transcendentals=0,
        ),
        name="expand",
    )(chosen, first, second, key_up, value_up, key_base, value_base)


def place_kernel(aliased, *refs):
    part_ref, out_ref, sem = refs[-3:]
    mine = lax.axis_index("team") & 1
    head = 1 - mine if aliased else mine
    copy = pltpu.make_async_copy(part_ref, out_ref.at[:, head], sem)
    copy.start()
    copy.wait()


def place(part, result, heads):
    tokens, group, head_dim = part.shape
    whole = pl.BlockSpec(memory_space=pl.ANY)
    operands = [part] if result is None else [result, part]
    return pl.pallas_call(
        functools.partial(place_kernel, result is not None),
        out_shape=jax.ShapeDtypeStruct((tokens, heads, group, head_dim), part.dtype),
        in_specs=[whole] * (len(operands) - 1) + [VMEM],
        out_specs=whole,
        scratch_shapes=[pltpu.SemaphoreType.DMA(())],
        input_output_aliases={} if result is None else {0: 0},
        compiler_params=pltpu.CompilerParams(vmem_limit_bytes=LIMIT),
        name="place",
    )(*operands)


def wide(value, width):
    return jnp.concatenate([value] * (width // value.shape[1]), axis=1)


def attend_kernel(span, masks, carried, final, group, scale, *refs):
    bound_ref, refs = (None, refs) if set(masks) == {None} else (refs[0], refs[1:])
    q_ref, refs = refs[0], refs[1:]
    state_refs, refs = refs[: 2 * carried], refs[2 * carried :]
    kv_refs, outs = refs[: len(masks)], refs[len(masks) :]
    head_dim = q_ref.shape[1]
    start, rows = span

    def body(i, _):
        here = pl.ds(pl.multiple_of(i * TILE, TILE), TILE)
        at = pl.ds(pl.multiple_of(start + i * TILE, TILE), TILE)
        q = q_ref[at, :]
        scores = []
        top = None
        for kv, mask in zip(kv_refs, masks):
            half = kv.shape[0] // 2
            s = dot_t(q, kv[:half, :])
            if mask is not None:
                limit = bound_ref[mask : mask + 1, :] * group + (start + i * TILE)
                ahead = lax.broadcasted_iota(jnp.int32, (TILE, half), 1) * group
                ahead = ahead - lax.broadcasted_iota(jnp.int32, (TILE, half), 0)
                s = jnp.where(ahead <= wide(limit, half), s, NEG_FILL)
            scores.append(s)
            most = jnp.max(s, axis=1, keepdims=True)
            top = most if top is None else jnp.maximum(top, most)
        top = jnp.broadcast_to(top * scale, (TILE, head_dim))
        acc = None
        if carried:
            old = state_refs[0][at, :]
            top = jnp.maximum(top, old)
            acc = state_refs[1][at, :] * wide(jnp.exp2(old - top), 2 * head_dim)
        for s, kv in zip(scores, kv_refs):
            half = kv.shape[0] // 2
            p = jnp.exp2(s * scale - wide(top, half))
            values = kv[half:, :]
            values = jnp.concatenate([values, jnp.ones_like(values)], axis=1)
            part = jnp.dot(p.astype(jnp.bfloat16), values, preferred_element_type=jnp.float32)
            acc = part if acc is None else acc + part
        if final:
            outs[0][here, :] = (acc[:, :head_dim] / acc[:, head_dim:]).astype(jnp.bfloat16)
        else:
            outs[0][here, :] = top
            outs[1][here, :] = acc
        return 0

    lax.fori_loop(0, rows // TILE, body, 0, unroll=min(UNROLL, rows // TILE))


def attend(bounds, queries, state, pieces, final, group, scale, span=None):
    span = span or (0, queries.shape[0])
    rows, head_dim = span[1], queries.shape[1]
    masks = tuple(mask for mask, _ in pieces)
    keys = sum(piece.shape[0] // 2 for _, piece in pieces)
    if final:
        shapes = [jax.ShapeDtypeStruct((rows, head_dim), jnp.bfloat16)]
    else:
        shapes = [
            jax.ShapeDtypeStruct((rows, head_dim), jnp.float32),
            jax.ShapeDtypeStruct((rows, 2 * head_dim), jnp.float32),
        ]
    operands = [queries, *(state or []), *(piece for _, piece in pieces)]
    table = [] if set(masks) == {None} else [bounds]
    return pl.pallas_call(
        functools.partial(attend_kernel, span, masks, state is not None, final, group, scale),
        out_shape=shapes,
        in_specs=[VMEM] * len(table + operands),
        out_specs=[VMEM] * len(shapes),
        compiler_params=pltpu.CompilerParams(vmem_limit_bytes=LIMIT),
        cost_estimate=pl.CostEstimate(
            flops=6 * rows * keys * head_dim,
            bytes_accessed=rows * head_dim * 4,
            transcendentals=rows * keys,
        ),
        name="attend",
    )(*table, *operands)


def butterfly(value, axis, size):
    step = 1
    pair = (value, None)
    while step < size:
        value = pair[0] if pair[1] is None else pair[0] + pair[1]
        perm = [(i, i ^ step) for i in range(size)]
        pair = (value, lax.ppermute(value, axis, perm))
        step *= 2
    return pair


def gather_blocks(value, count, before=None):
    held = {0: value}
    step = count // 2
    while step:
        perm = [(i, i ^ step) for i in range(count)]
        for mask in list(held):
            sent = held[mask]
            if before is not None and (mask ^ step) == count - 1:
                sent, before = lax.optimization_barrier((sent, before))
            held[mask ^ step] = lax.ppermute(sent, "blk", perm)
        step //= 2
    return held, before


def on_device(
    queries,
    features,
    adapter_down,
    adapter_key_up,
    adapter_value_up,
    base_key,
    base_value,
    prefix_key,
    prefix_value,
    adapter_ids,
    block_order,
):
    block_count = lax.axis_size("blk")
    team_count = lax.axis_size("team")
    query_dev, kv_heads, group_dev, head_dim = queries.shape
    mine = lax.axis_index("team") & 1
    scale = LOG2E / math.sqrt(head_dim)
    rows = query_dev * group_dev

    def swap(value):
        return lax.ppermute(value, "team", [(i, i ^ 1) for i in range(team_count)])

    def pick(array, axis, other=False):
        index = 1 - mine if other else mine
        return lax.dynamic_index_in_dim(array, index, axis, keepdims=False)

    latent, bounds, chosen = partial_latent(adapter_ids, block_order, features, jnp.swapaxes(adapter_down, 1, 2))
    own_prefix = pick(jnp.concatenate([prefix_key, prefix_value], axis=0), 1)
    first, second = butterfly(latent, "head", lax.axis_size("head"))
    first, second = butterfly(first + second, "team", team_count)

    prefix, _ = gather_blocks(own_prefix, block_count)
    own_queries = pick(queries, 1).reshape(rows, head_dim)
    far_queries = swap(pick(queries, 1, True).reshape(rows, head_dim))
    own_new = expand(
        chosen,
        first,
        second,
        pick(adapter_key_up, 2),
        pick(adapter_value_up, 2),
        pick(base_key, 1),
        pick(base_value, 1),
    )
    last = block_count - 1
    early = [(None, piece) for mask, piece in prefix.items() if mask != last]
    own_state = attend(bounds, own_queries, None, early, False, group_dev, scale)
    new, own_state = gather_blocks(own_new, block_count, own_state)
    far_state = attend(bounds, far_queries, None, early, False, group_dev, scale)
    half = block_count // 2
    relayed = [(None, prefix[last])]
    middle = [(mask, new[mask]) for mask in new if mask in (0, half)]
    tail = [(mask, new[mask]) for mask in new if mask not in (0, half)]
    own_state = attend(bounds, own_queries, own_state, middle, False, group_dev, scale)
    far_state = attend(bounds, far_queries, far_state, middle + relayed, False, group_dev, scale)
    far_state, own_state = lax.optimization_barrier((far_state, own_state))
    near = [(mask, piece) for mask, piece in tail if mask != last]
    far_state = attend(bounds, far_queries, far_state, near, False, group_dev, scale)
    parts = 1
    part = rows // parts
    received = []
    for n in range(parts):
        span = (n * part, part)
        out = attend(bounds, far_queries, far_state, tail[-1:], True, group_dev, scale, span)[0]
        received.append(swap(out))
    own_out = attend(bounds, own_queries, own_state, relayed + tail, True, group_dev, scale)[0]
    shape = (query_dev, group_dev, head_dim)
    result = place(own_out.reshape(shape), None, kv_heads)
    return place(received[0].reshape(shape), result, kv_heads)


def solution(mesh):
    placed = (
        P("blk", "head", "team", None),
        P("blk", ("team", "head")),
        P(None, ("team", "head"), None),
        P(None, None, "head", None),
        P(None, None, "head", None),
        P("blk", "head", None),
        P("blk", "head", None),
        P("blk", "head", None),
        P("blk", "head", None),
        P(),
        P(),
    )

    return jax.shard_map(
        on_device,
        mesh=mesh,
        in_specs=placed,
        out_specs=P("blk", "head", "team", None),
        check_vma=False,
    )
```

```python
import functools
import math

import jax
import jax.numpy as jnp
from jax import lax
from jax.experimental import pallas as pl
from jax.experimental.pallas import tpu as pltpu
from jax.sharding import PartitionSpec as P


NEG_FILL = -1e30
LOG2E = 1.4426950408889634
TILE = 128
UNROLL = 8
LIMIT = 20 * 2**20
VMEM = pl.BlockSpec(memory_space=pltpu.VMEM)
SMEM = pl.BlockSpec(memory_space=pltpu.SMEM)


def dot_t(a, b):
    return lax.dot_general(a, b, (((1,), (1,)), ((), ())), preferred_element_type=jnp.float32)


def latent_kernel(ids_ref, order_ref, features_ref, down_ref, out_ref, bound_ref, chosen_ref):
    me = lax.axis_index("blk")
    chosen = ids_ref[me]
    out_ref[...] = dot_t(down_ref[chosen], features_ref[...])
    tokens = features_ref.shape[0]
    lanes = (1, bound_ref.shape[1])
    for mask in range(order_ref.shape[0]):
        bound = (order_ref[me] - order_ref[me ^ mask]) * tokens
        bound_ref[mask : mask + 1, :] = jnp.full(lanes, bound, jnp.int32)
    for adapter in range(down_ref.shape[0]):
        chosen_ref[adapter : adapter + 1, :] = jnp.full(lanes, chosen - adapter, jnp.int32)


def partial_latent(ids, order, features, down):
    tokens, depth = features.shape
    adapters, rank, _ = down.shape
    return pl.pallas_call(
        latent_kernel,
        out_shape=[
            jax.ShapeDtypeStruct((rank, tokens), jnp.float32),
            jax.ShapeDtypeStruct((order.shape[0], 128), jnp.int32),
            jax.ShapeDtypeStruct((adapters, 128), jnp.int32),
        ],
        in_specs=[SMEM, SMEM, VMEM, VMEM],
        out_specs=[VMEM] * 3,
        compiler_params=pltpu.CompilerParams(vmem_limit_bytes=LIMIT),
        cost_estimate=pl.CostEstimate(
            flops=2 * tokens * depth * rank,
            bytes_accessed=2 * depth * (tokens + rank),
            transcendentals=0,
        ),
        name="partial_latent",
    )(ids, order, features, down)


def expand_kernel(chosen_ref, first, second, key_up, value_up, key_base, value_base, out_ref):
    latent = (first[...] + second[...]).astype(jnp.bfloat16)
    tokens = key_base.shape[0]
    for n, (up, base) in enumerate(((key_up, key_base), (value_up, value_base))):
        delta = None
        for adapter in range(up.shape[0]):
            term = lax.dot_general(
                latent, up[adapter], (((0,), (0,)), ((), ())), preferred_element_type=jnp.float32
            )
            here = chosen_ref[adapter : adapter + 1, : term.shape[1]] == 0
            delta = term if delta is None else jnp.where(here, term, delta)
        out_ref[n * tokens : (n + 1) * tokens, :] = (
            base[...].astype(jnp.float32) + delta
        ).astype(jnp.bfloat16)


def expand(chosen, first, second, key_up, value_up, key_base, value_base):
    tokens, head_dim = key_base.shape
    return pl.pallas_call(
        expand_kernel,
        out_shape=jax.ShapeDtypeStruct((2 * tokens, head_dim), jnp.bfloat16),
        in_specs=[VMEM] * 7,
        out_specs=VMEM,
        compiler_params=pltpu.CompilerParams(vmem_limit_bytes=LIMIT),
        cost_estimate=pl.CostEstimate(
            flops=4 * tokens * head_dim * first.shape[0],
            bytes_accessed=8 * tokens * head_dim,
            transcendentals=0,
        ),
        name="expand",
    )(chosen, first, second, key_up, value_up, key_base, value_base)


def place_kernel(aliased, *refs):
    part_ref, out_ref, sem = refs[-3:]
    mine = lax.axis_index("team") & 1
    head = 1 - mine if aliased else mine
    copy = pltpu.make_async_copy(part_ref, out_ref.at[:, head], sem)
    copy.start()
    copy.wait()


def place(part, result, heads):
    tokens, group, head_dim = part.shape
    whole = pl.BlockSpec(memory_space=pl.ANY)
    operands = [part] if result is None else [result, part]
    return pl.pallas_call(
        functools.partial(place_kernel, result is not None),
        out_shape=jax.ShapeDtypeStruct((tokens, heads, group, head_dim), part.dtype),
        in_specs=[whole] * (len(operands) - 1) + [VMEM],
        out_specs=whole,
        scratch_shapes=[pltpu.SemaphoreType.DMA(())],
        input_output_aliases={} if result is None else {0: 0},
        compiler_params=pltpu.CompilerParams(vmem_limit_bytes=LIMIT),
        name="place",
    )(*operands)


def wide(value, width):
    return jnp.concatenate([value] * (width // value.shape[1]), axis=1)


def attend_kernel(span, masks, carried, final, group, scale, *refs):
    bound_ref, refs = (None, refs) if set(masks) == {None} else (refs[0], refs[1:])
    q_ref, refs = refs[0], refs[1:]
    state_refs, refs = refs[: 2 * carried], refs[2 * carried :]
    kv_refs, outs = refs[: len(masks)], refs[len(masks) :]
    head_dim = q_ref.shape[1]
    start, rows = span

    def body(i, _):
        here = pl.ds(pl.multiple_of(i * TILE, TILE), TILE)
        at = pl.ds(pl.multiple_of(start + i * TILE, TILE), TILE)
        q = q_ref[at, :]
        scores = []
        top = None
        for kv, mask in zip(kv_refs, masks):
            half = kv.shape[0] // 2
            s = dot_t(q, kv[:half, :])
            if mask is not None:
                limit = bound_ref[mask : mask + 1, :] * group + (start + i * TILE)
                ahead = lax.broadcasted_iota(jnp.int32, (TILE, half), 1) * group
                ahead = ahead - lax.broadcasted_iota(jnp.int32, (TILE, half), 0)
                s = jnp.where(ahead <= wide(limit, half), s, NEG_FILL)
            scores.append(s)
            most = jnp.max(s, axis=1, keepdims=True)
            top = most if top is None else jnp.maximum(top, most)
        top = jnp.broadcast_to(top * scale, (TILE, head_dim))
        acc = None
        if carried:
            old = state_refs[0][at, :]
            top = jnp.maximum(top, old)
            acc = state_refs[1][at, :] * wide(jnp.exp2(old - top), 2 * head_dim)
        for s, kv in zip(scores, kv_refs):
            half = kv.shape[0] // 2
            p = jnp.exp2(s * scale - wide(top, half))
            values = kv[half:, :]
            values = jnp.concatenate([values, jnp.ones_like(values)], axis=1)
            part = jnp.dot(p.astype(jnp.bfloat16), values, preferred_element_type=jnp.float32)
            acc = part if acc is None else acc + part
        if final:
            outs[0][here, :] = (acc[:, :head_dim] / acc[:, head_dim:]).astype(jnp.bfloat16)
        else:
            outs[0][here, :] = top
            outs[1][here, :] = acc
        return 0

    lax.fori_loop(0, rows // TILE, body, 0, unroll=min(UNROLL, rows // TILE))


def attend(bounds, queries, state, pieces, final, group, scale, span=None):
    span = span or (0, queries.shape[0])
    rows, head_dim = span[1], queries.shape[1]
    masks = tuple(mask for mask, _ in pieces)
    keys = sum(piece.shape[0] // 2 for _, piece in pieces)
    if final:
        shapes = [jax.ShapeDtypeStruct((rows, head_dim), jnp.bfloat16)]
    else:
        shapes = [
            jax.ShapeDtypeStruct((rows, head_dim), jnp.float32),
            jax.ShapeDtypeStruct((rows, 2 * head_dim), jnp.float32),
        ]
    operands = [queries, *(state or []), *(piece for _, piece in pieces)]
    table = [] if set(masks) == {None} else [bounds]
    return pl.pallas_call(
        functools.partial(attend_kernel, span, masks, state is not None, final, group, scale),
        out_shape=shapes,
        in_specs=[VMEM] * len(table + operands),
        out_specs=[VMEM] * len(shapes),
        compiler_params=pltpu.CompilerParams(vmem_limit_bytes=LIMIT),
        cost_estimate=pl.CostEstimate(
            flops=6 * rows * keys * head_dim,
            bytes_accessed=rows * head_dim * 4,
            transcendentals=rows * keys,
        ),
        name="attend",
    )(*table, *operands)


def latent_pair(value):
    heads, teams = lax.axis_size("head"), lax.axis_size("team")
    steps = [("head", 1 << n) for n in range(heads.bit_length() - 1)]
    steps[1:1] = [("team", 1 << n) for n in range(teams.bit_length() - 1)]
    received = None
    for axis, step in steps:
        value = value if received is None else value + received
        perm = [(i, i ^ step) for i in range(lax.axis_size(axis))]
        received = lax.ppermute(value, axis, perm)
    return value, received


def gather_blocks(value, count, before=None):
    held = {0: value}
    step = count // 2
    while step:
        perm = [(i, i ^ step) for i in range(count)]
        for mask in list(held):
            sent = held[mask]
            if before is not None and (mask ^ step) == count - 1:
                sent, before = lax.optimization_barrier((sent, before))
            held[mask ^ step] = lax.ppermute(sent, "blk", perm)
        step //= 2
    return held, before


def on_device(
    queries,
    features,
    adapter_down,
    adapter_key_up,
    adapter_value_up,
    base_key,
    base_value,
    prefix_key,
    prefix_value,
    adapter_ids,
    block_order,
):
    block_count = lax.axis_size("blk")
    team_count = lax.axis_size("team")
    query_dev, kv_heads, group_dev, head_dim = queries.shape
    mine = lax.axis_index("team") & 1
    scale = LOG2E / math.sqrt(head_dim)
    rows = query_dev * group_dev

    def swap(value):
        return lax.ppermute(value, "team", [(i, i ^ 1) for i in range(team_count)])

    def pick(array, axis, other=False):
        index = 1 - mine if other else mine
        return lax.dynamic_index_in_dim(array, index, axis, keepdims=False)

    latent, bounds, chosen = partial_latent(adapter_ids, block_order, features, jnp.swapaxes(adapter_down, 1, 2))
    own_prefix = pick(jnp.concatenate([prefix_key, prefix_value], axis=0), 1)
    first, second = latent_pair(latent)
    prefix, _ = gather_blocks(own_prefix, block_count)
    own_queries = pick(queries, 1).reshape(rows, head_dim)
    far_queries = swap(pick(queries, 1, True).reshape(rows, head_dim))
    own_new = expand(
        chosen,
        first,
        second,
        pick(adapter_key_up, 2),
        pick(adapter_value_up, 2),
        pick(base_key, 1),
        pick(base_value, 1),
    )
    last = block_count - 1
    early = [(None, piece) for mask, piece in prefix.items() if mask != last]
    own_state = attend(bounds, own_queries, None, early, False, group_dev, scale)
    new, own_state = gather_blocks(own_new, block_count, own_state)
    far_state = attend(bounds, far_queries, None, early, False, group_dev, scale)
    half = block_count // 2
    relayed = [(None, prefix[last])]
    middle = [(mask, new[mask]) for mask in new if mask in (0, half)]
    tail = [(mask, new[mask]) for mask in new if mask not in (0, half)]
    far_state = attend(bounds, far_queries, far_state, middle + relayed, False, group_dev, scale)
    far_state, own_state = lax.optimization_barrier((far_state, own_state))
    near = [(mask, piece) for mask, piece in tail if mask != last]
    far_state = attend(bounds, far_queries, far_state, near, False, group_dev, scale)
    parts = 1
    part = rows // parts
    received = []
    for n in range(parts):
        span = (n * part, part)
        out = attend(bounds, far_queries, far_state, tail[-1:], True, group_dev, scale, span)[0]
        received.append(swap(out))
    own_out = attend(bounds, own_queries, own_state, relayed + middle + tail, True, group_dev, scale)[0]
    shape = (query_dev, group_dev, head_dim)
    result = place(own_out.reshape(shape), None, kv_heads)
    return place(received[0].reshape(shape), result, kv_heads)


def solution(mesh):
    placed = (
        P("blk", "head", "team", None),
        P("blk", ("team", "head")),
        P(None, ("team", "head"), None),
        P(None, None, "head", None),
        P(None, None, "head", None),
        P("blk", "head", None),
        P("blk", "head", None),
        P("blk", "head", None),
        P("blk", "head", None),
        P(),
        P(),
    )

    return jax.shard_map(
        on_device,
        mesh=mesh,
        in_specs=placed,
        out_specs=P("blk", "head", "team", None),
        check_vma=False,
    )
```
